256 devices in a mesh: dp: 16 (over y, x_lo, core), seq: 16 (over z, x_hi).
Axes of the slice: x: 4 (x_hi: 2, x_lo: 2; x = x_hi * 2 + x_lo), y: 4, z: 8, core: 2. Of those that a mesh axis runs over, the one named last changes fastest.
Arguments:
- queries: bfloat16 [131072, 1536], P(('dp', 'seq')), may hold values from -8 to 8
- keys: bfloat16 [131072, 1536], P(('dp', 'seq')), may hold values from -8 to 8
- values: bfloat16 [131072, 1536], P(('dp', 'seq')), may hold values from -6 to 6
- grad_out: bfloat16 [131072, 1536], P(('dp', 'seq')), may hold values from -24 to 24
- out_weight: bfloat16 [1536, 1536], P('dp'), may hold values from -0.15625 to 0.15625
- lengths: int32 [16], P('dp'), may hold values from 1024 to 8192, as said below
Outputs:
- grad_queries: bfloat16 [131072, 1536], P(('dp', 'seq'))
- grad_keys: bfloat16 [131072, 1536], P(('dp', 'seq'))
- grad_values: bfloat16 [131072, 1536], P(('dp', 'seq'))
- grad_weight: float32 [1536, 1536], P(('dp', 'seq'))
The draws below stay inside these ranges and needn't reach their ends.
Inputs may be any that keep to these rules, and one draw needn't show every extreme that they name: `lengths`: every draw holds one stretch of 8192 valid bytes and one of 1024.
All inputs are finite; a program needn't handle non-finite values.
Results may differ from the reference program's by a relative error of at most 0.0058.
Values may be sent and summed in bfloat16 or wider, within the bound.
No kernel may reach another device: no remote copies, remote signals or barrier semaphores. Data moves between devices by JAX's collectives and lax.ppermute only.
A program may use at most 192 MiB of HBM per device.

```python
import jax
import jax.numpy as jnp
from jax import lax

HEADS = 12
HEAD_DIM = 128
D = 1536
WINDOW = 512
TOK_DEV = 512
DOC = 8192
DOCS = 16
TOKENS = 131072


def drawn_pair(base_key):
    seeded = jax.random.fold_in(base_key, 11)
    key_query, key_keys = jax.random.split(seeded, 2)
    query_vals = jax.random.normal(key_query, (TOKENS, D), jnp.float32)
    key_vals = jax.random.normal(key_keys, (TOKENS, D), jnp.float32)
    return (jnp.clip(query_vals, -8.0, 8.0), jnp.clip(key_vals, -8.0, 8.0))


def draw_queries(key, part):
    return drawn_pair(key)[0].astype(jnp.bfloat16)


def draw_keys(key, part):
    return drawn_pair(key)[1].astype(jnp.bfloat16)


def draw_lengths(key, part):
    key_base, key_order = jax.random.split(jax.random.fold_in(key, 23))
    drawn = jax.random.randint(key_base, (DOCS,), DOC // 8, DOC + 1)
    order = jax.random.permutation(key_order, DOCS)
    drawn = drawn.at[order[0]].set(DOC)
    drawn = drawn.at[order[1]].set(DOC // 8)
    return drawn.astype(jnp.int32)


def strengthened(values, rng, source, target, parts, factor):
    owner, partner = [(jnp.arange(values.shape[dim]) // (values.shape[dim] // parts)).reshape([-1 if axis == dim else 1 for axis in range(values.ndim)]) for dim in (source, target)]
    chosen = jax.random.permutation(rng, parts)[partner]
    strong = (owner == chosen) | (owner == (partner + parts // 2) % parts)
    return jnp.where(strong, factor * values, values)


def levels(stream_key, dims, cuts, low, largest):
    def one(dim, parts):
        steps = jax.random.uniform(jax.random.fold_in(jax.random.fold_in(stream_key, 6), dim), (parts,), jnp.float32, low / len(cuts), largest / len(cuts))
        return jnp.repeat(jnp.exp(steps), dims[dim] // parts).reshape((-1,) + (1,) * (len(dims) - dim - 1))

    loudness = one(*cuts[0])
    for cut in cuts[1:]:
        loudness = loudness * one(*cut)
    return loudness


def bell_draw(own_key, shape, scale, limit, shards=(), kind=jnp.bfloat16):
    values = jax.random.normal(own_key, shape, jnp.float32) * scale
    if len(shards) > 0:
        values = levels(own_key, shape, shards, -0.22, 0.18) * values
    return jnp.clip(values, min=-limit, max=limit).astype(kind)


def heavy_noise(stream_key, extent, spread, reach, pieces, heavy, kind=jnp.bfloat16):
    values = spread * jax.random.normal(stream_key, extent, jnp.float32)
    if pieces:
        values = values * levels(stream_key, extent, pieces, -0.22, 0.18)
    return jnp.clip(strengthened(values, jax.random.fold_in(stream_key, 3), *heavy), -reach, reach).astype(kind)


def setup_inputs(seed: int = 0) -> dict:
    key_list = jax.random.split(jax.random.key(seed), 7)
    return {
        "queries": draw_queries(jax.random.fold_in(key_list[6], 71), 0),
        "keys": draw_keys(jax.random.fold_in(key_list[6], 71), 0),
        "values": bell_draw(key_list[2], (TOKENS, D), 1.0, 6.0, ((0, 256),)),
        "grad_out": heavy_noise(key_list[3], (TOKENS, D), 1.0, 24.0, ((0, 256),), (0, 1, 256, 6.0)),
        "out_weight": bell_draw(key_list[4], (D, D), D ** -0.5, 0.15625, ((0, 16),)),
        "lengths": draw_lengths(jax.random.fold_in(key_list[6], 71), 0),
    }


def window_backward(query_block, key_window, value_window, grad_block, query_pos, key_pos, length):
    half_window = WINDOW // 2
    inv_root = HEAD_DIM ** -0.5
    offset = key_pos[None, :] - query_pos[:, None]
    allowed = (offset >= -half_window) & (offset < half_window)
    allowed = allowed & (key_pos[None, :] >= 0) & (key_pos[None, :] < length) & (query_pos[:, None] < length)

    def split_heads(matrix):
        return matrix.reshape(matrix.shape[0], HEADS, HEAD_DIM).transpose(1, 0, 2)

    def join_heads(stacked):
        return stacked.transpose(1, 0, 2).reshape(stacked.shape[1], HEADS * HEAD_DIM)

    def one_head(operands):
        query_head, key_head, value_head, grad_head = operands
        scores = lax.dot_general(query_head, key_head, (((1,), (1,)), ((), ())), preferred_element_type=jnp.float32) * inv_root
        scores = jnp.where(allowed, scores, -1e30)
        row_max = jnp.max(scores, axis=1, keepdims=True)
        expo = jnp.where(allowed, jnp.exp(scores - row_max), 0.0)
        row_total = jnp.maximum(jnp.sum(expo, axis=1, keepdims=True), 1.0)
        probability = expo / row_total
        probability_b = probability.astype(jnp.bfloat16)
        attended_head = jnp.dot(probability_b, value_head, preferred_element_type=jnp.float32)
        grad_probs = lax.dot_general(grad_head, value_head, (((1,), (1,)), ((), ())), preferred_element_type=jnp.float32)
        row_delta = jnp.sum(probability * grad_probs, axis=1, keepdims=True)
        grad_scores = (probability * (grad_probs - row_delta) * inv_root).astype(jnp.bfloat16)
        grad_query = jnp.dot(grad_scores, key_head, preferred_element_type=jnp.float32)
        grad_key = lax.dot_general(grad_scores, query_head, (((0,), (0,)), ((), ())), preferred_element_type=jnp.float32)
        grad_value = lax.dot_general(probability_b, grad_head, (((0,), (0,)), ((), ())), preferred_element_type=jnp.float32)
        return attended_head, grad_query, grad_key, grad_value

    outputs = lax.map(one_head, (split_heads(query_block), split_heads(key_window), split_heads(value_window), split_heads(grad_block)))
    attended_heads, grad_query, grad_key, grad_value = outputs
    return join_heads(attended_heads).astype(jnp.bfloat16), join_heads(grad_query), join_heads(grad_key), join_heads(grad_value)


def reference(queries, keys, values, grad_out, out_weight, lengths):
    half_window = WINDOW // 2
    block_count = DOC // TOK_DEV
    window_rows = TOK_DEV + 2 * half_window

    def single_document(operands):
        doc_query, doc_keys, doc_values, doc_grad, length = operands
        grad_mixed = jnp.dot(doc_grad, out_weight, preferred_element_type=jnp.float32).astype(jnp.bfloat16)
        zero_rows = jnp.zeros((half_window, D), jnp.bfloat16)
        keys_padded = jnp.concatenate([zero_rows, doc_keys, zero_rows], axis=0)
        values_padded = jnp.concatenate([zero_rows, doc_values, zero_rows], axis=0)

        def block_step(accumulator, block_index):
            first_row = (block_index * TOK_DEV).astype(jnp.int32)
            query_block = lax.dynamic_slice_in_dim(doc_query, first_row, TOK_DEV, 0)
            key_window = lax.dynamic_slice_in_dim(keys_padded, first_row, window_rows, 0)
            value_window = lax.dynamic_slice_in_dim(values_padded, first_row, window_rows, 0)
            grad_block = lax.dynamic_slice_in_dim(grad_mixed, first_row, TOK_DEV, 0)
            query_pos = first_row + jnp.arange(TOK_DEV, dtype=jnp.int32)
            key_pos = first_row - half_window + jnp.arange(window_rows, dtype=jnp.int32)
            attended, grad_query, grad_key, grad_value = window_backward(query_block, key_window, value_window, grad_block, query_pos, key_pos, length)
            paired = jnp.stack([grad_key, grad_value])
            current = lax.dynamic_slice_in_dim(accumulator, first_row, window_rows, 1)
            accumulator = lax.dynamic_update_slice_in_dim(accumulator, current + paired, first_row, 1)
            return accumulator, (attended, grad_query)

        start_acc = jnp.zeros((2, DOC + 2 * half_window, D), jnp.float32)
        accumulator, (attended, grad_query) = lax.scan(block_step, start_acc, jnp.arange(block_count, dtype=jnp.int32))
        attended = attended.reshape(DOC, D)
        grad_query = grad_query.reshape(DOC, D).astype(jnp.bfloat16)
        key_value = accumulator[:, half_window:half_window + DOC].astype(jnp.bfloat16)
        weight_part = lax.dot_general(doc_grad, attended, (((0,), (0,)), ((), ())), preferred_element_type=jnp.float32)
        return grad_query, key_value[0], key_value[1], weight_part

    def shaped(matrix):
        return matrix.reshape(DOCS, DOC, D)

    grad_query, grad_key, grad_value, weight_parts = lax.map(single_document, (shaped(queries), shaped(keys), shaped(values), shaped(grad_out), lengths))
    return (grad_query.reshape(TOKENS, D), grad_key.reshape(TOKENS, D), grad_value.reshape(TOKENS, D), jnp.sum(weight_parts, axis=0))
```

```python
import jax
import jax.numpy as jnp
from jax import lax
from jax.experimental import pallas as pl
from jax.experimental.pallas import tpu as pltpu
from jax.sharding import PartitionSpec as P

HEAD_DIM = 128
HALF = 256
LOG2E = 1.4426950408889634


def dot_nt(a, b):
    return lax.dot_general(a, b, (((1,), (1,)), ((), ())), preferred_element_type=jnp.float32)


def dot_nn(a, b):
    return lax.dot_general(a, b, (((1,), (0,)), ((), ())), preferred_element_type=jnp.float32)


def dot_tn(a, b):
    return lax.dot_general(a, b, (((0,), (0,)), ((), ())), preferred_element_type=jnp.float32)


def attention_kernel(
    meta, q, k, v, gm, kl, vl, kr, vr, att, dq, dk, dv, dkl, dvl, dkr, dvr, bias
):
    rows = q.shape[0]
    width = 3 * HALF
    scale = HEAD_DIM ** (-0.5)
    first_row = meta[0]
    length = meta[1]

    @pl.when(pl.program_id(0) == 0)
    def _():
        for b in range(rows // HALF):
            start = first_row + b * HALF
            r = lax.broadcasted_iota(jnp.int32, (HALF, width), 0)
            c = lax.broadcasted_iota(jnp.int32, (HALF, width), 1)
            u = c + (start - HALF)
            ok = (c >= r) & (c < r + 2 * HALF) & (u >= 0) & (u < length)
            bias[b] = jnp.where(ok, 0.0, -1e30)

    k_all = [kl[...], k[0:HALF], k[HALF : 2 * HALF], kr[...]]
    v_all = [vl[...], v[0:HALF], v[HALF : 2 * HALF], vr[...]]
    dks, dvs = [], []
    for b in range(rows // HALF):
        lo, hi = b * HALF, (b + 1) * HALF
        qb, gb = q[lo:hi], gm[lo:hi]
        kc = jnp.concatenate(k_all[b : b + 3], axis=0)
        vc = jnp.concatenate(v_all[b : b + 3], axis=0)
        s = dot_nt(qb, kc) + bias[b]
        dp = dot_nt(gb, vc)
        m = jnp.max(s, axis=1, keepdims=True)
        e = jnp.exp2((s - m) * (scale * LOG2E))
        pos = first_row + lo + lax.broadcasted_iota(jnp.int32, (HALF, 1), 0)
        total = jnp.maximum(jnp.sum(e, axis=1, keepdims=True), 1.0)
        inv = jnp.where(pos < length, 1.0 / total, 0.0)
        p = e * inv
        pb = p.astype(jnp.bfloat16)
        att[lo:hi] = dot_nn(pb, vc).astype(att.dtype)
        delta = jnp.sum(p * dp, axis=1, keepdims=True)
        ds = (p * (dp - delta) * scale).astype(jnp.bfloat16)
        dq[lo:hi] = dot_nn(ds, kc).astype(dq.dtype)
        dks.append(dot_tn(ds, qb))
        dvs.append(dot_tn(pb, gb))
    for parts, left, own, right in ((dks, dkl, dk, dkr), (dvs, dvl, dv, dvr)):
        a, b = parts
        left[...] = a[0:HALF].astype(left.dtype)
        own[0:HALF] = (a[HALF : 2 * HALF] + b[0:HALF]).astype(own.dtype)
        own[HALF : 2 * HALF] = (a[2 * HALF :] + b[HALF : 2 * HALF]).astype(own.dtype)
        right[...] = b[2 * HALF :].astype(right.dtype)


def attention(meta, q, k, v, gm, kl, vl, kr, vr, heads=12, off=0):
    rows = q.shape[0]
    f32, bf16 = jnp.float32, jnp.bfloat16

    def whole(n, o=0):
        return pl.BlockSpec((n, HEAD_DIM), lambda h, s: (0, h + o))

    sds = jax.ShapeDtypeStruct
    w = heads * HEAD_DIM
    return pl.pallas_call(
        attention_kernel,
        name="attention",
        out_shape=[
            sds((rows, w), bf16),
            sds((rows, w), bf16),
            sds((rows, w), f32),
            sds((rows, w), f32),
            sds((HALF, w), bf16),
            sds((HALF, w), bf16),
            sds((HALF, w), bf16),
            sds((HALF, w), bf16),
        ],
        grid_spec=pltpu.PrefetchScalarGridSpec(
            num_scalar_prefetch=1,
            grid=(heads,),
            in_specs=[whole(rows, off)] * 3 + [whole(rows)] + [whole(HALF)] * 4,
            out_specs=[whole(rows)] * 4 + [whole(HALF)] * 4,
            scratch_shapes=[pltpu.VMEM((rows // HALF, HALF, 3 * HALF), f32)],
        ),
        compiler_params=pltpu.CompilerParams(dimension_semantics=("arbitrary",)),
    )(meta, q, k, v, gm, kl, vl, kr, vr)


def passed(value, axis, by):
    devices = lax.axis_size(axis)
    pairs = [(i, i + by) for i in range(devices) if 0 <= i + by < devices]
    return lax.ppermute(value, axis, pairs)


def halved(value, axis, bit, dim):
    mine = (lax.axis_index(axis) // bit) % 2 == 1
    low = lax.slice_in_dim(value, 0, 1, axis=dim)
    high = lax.slice_in_dim(value, 1, 2, axis=dim)
    pairs = [(i, i ^ bit) for i in range(lax.axis_size(axis))]
    sent = jnp.where(mine, low, high).astype(jnp.bfloat16)
    return jnp.where(mine, high, low) + lax.ppermute(sent, axis, pairs).astype(jnp.float32)


def scattered(part):
    cols = part.shape[1]
    part = part.reshape(2, 2, 2, 2, -1, cols)
    for bit, dim in ((1, 3), (4, 1), (8, 0)):
        part = halved(part, "dp", bit, dim)
    part = part.reshape(2, 2, 2, 2, 2, -1, cols)
    for axis, bit, dim in (("seq", 2, 3), ("seq", 4, 2), ("seq", 8, 1), ("dp", 2, 0), ("seq", 1, 4)):
        part = halved(part, axis, bit, dim)
    return part.reshape(-1, cols)


def shards(queries, keys, values, grad_out, out_weight, lengths):
    rows, width = queries.shape
    f32, bf16 = jnp.float32, jnp.bfloat16
    first_row = lax.axis_index("seq") * rows
    meta = jnp.stack([first_row, lengths[0]]).astype(jnp.int32)
    kl = passed(keys[rows - HALF :], "seq", 1)
    vl = passed(values[rows - HALF :], "seq", 1)
    kr = passed(keys[:HALF], "seq", -1)
    vr = passed(values[:HALF], "seq", -1)
    weight = lax.all_gather(out_weight, "dp", axis=0, tiled=True)
    grad_mixed = jnp.dot(grad_out, weight, preferred_element_type=f32).astype(bf16)
    att, dq, dk, dv, dkl, dvl, dkr, dvr = attention(
        meta, queries, keys, values, grad_mixed, kl, vl, kr, vr, heads=width // HEAD_DIM
    )
    outs = []
    for own, left, right in ((dk, dkl, dkr), (dv, dvl, dvr)):
        low = passed(right, "seq", 1).astype(f32)
        high = passed(left, "seq", -1).astype(f32)
        outs.append((own + jnp.concatenate([low, high], axis=0)).astype(bf16))
    part = lax.dot_general(
        grad_out, att, (((0,), (0,)), ((), ())), preferred_element_type=f32
    )
    return dq, outs[0], outs[1], scattered(part)


def solution(mesh):
    rows = P(("dp", "seq"), None)
    return jax.shard_map(
        shards,
        mesh=mesh,
        in_specs=(rows, rows, rows, rows, P("dp", None), P("dp")),
        out_specs=(rows, rows, rows, rows),
        check_vma=False,
    )
```

```python
import jax
import jax.numpy as jnp
from jax import lax
from jax.experimental import pallas as pl
from jax.experimental.pallas import tpu as pltpu
from jax.sharding import PartitionSpec as P


HEAD_DIM = 128
HALF = 256
LOG2E = 1.4426950408889634
F32 = jnp.float32
BF16 = jnp.bfloat16
ANY = pl.BlockSpec(memory_space=pl.ANY)
SDS = jax.ShapeDtypeStruct


def dot_nt(a, b):
    return lax.dot_general(a, b, (((1,), (1,)), ((), ())), preferred_element_type=F32)


def dot_nn(a, b):
    return lax.dot_general(a, b, (((1,), (0,)), ((), ())), preferred_element_type=F32)


def dot_tn(a, b):
    return lax.dot_general(a, b, (((0,), (0,)), ((), ())), preferred_element_type=F32)


def attention_kernel(meta, q, k, v, gm, left, right, *refs):
    att, dq, dk, dv, gl, gr, bias = refs[-7:]
    rows = q.shape[0]
    width = 3 * HALF
    scale = HEAD_DIM ** (-0.5)
    first_row = meta[0]
    length = meta[1]

    @pl.when(pl.program_id(0) == 0)
    def _():
        for b in range(rows // HALF):
            start = first_row + b * HALF
            r = lax.broadcasted_iota(jnp.int32, (HALF, width), 0)
            c = lax.broadcasted_iota(jnp.int32, (HALF, width), 1)
            u = c + (start - HALF)
            ok = (c >= r) & (c < r + 2 * HALF) & (u >= 0) & (u < length)
            bias[b] = jnp.where(ok, 0.0, -1e30)

    k_all = [left[0], k[0:HALF], k[HALF : 2 * HALF], right[0]]
    v_all = [left[1], v[0:HALF], v[HALF : 2 * HALF], right[1]]
    dks, dvs = [], []
    for b in range(rows // HALF):
        lo, hi = b * HALF, (b + 1) * HALF
        qb, gb = q[lo:hi], gm[lo:hi]
        kc = jnp.concatenate(k_all[b : b + 3], axis=0)
        vc = jnp.concatenate(v_all[b : b + 3], axis=0)
        s = dot_nt(qb, kc) + bias[b]
        dp = dot_nt(gb, vc)
        m = jnp.max(s, axis=1, keepdims=True)
        e = jnp.exp2((s - m) * (scale * LOG2E))
        pos = first_row + lo + lax.broadcasted_iota(jnp.int32, (HALF, 1), 0)
        total = jnp.maximum(jnp.sum(e, axis=1, keepdims=True), 1.0)
        inv = jnp.where(pos < length, 1.0 / total, 0.0)
        p = e * inv
        pb = p.astype(BF16)
        att[lo:hi] = dot_nn(pb, vc).astype(att.dtype)
        delta = jnp.sum(p * dp, axis=1, keepdims=True)
        ds = (p * (dp - delta) * scale).astype(BF16)
        dq[lo:hi] = dot_nn(ds, kc).astype(dq.dtype)
        dks.append(dot_tn(ds, qb))
        dvs.append(dot_tn(pb, gb))
    for n, (parts, own) in enumerate(((dks, dk), (dvs, dv))):
        a, b = parts
        gl[n] = a[0:HALF].astype(gl.dtype)
        own[0:HALF] = a[HALF : 2 * HALF] + b[0:HALF]
        own[HALF : 2 * HALF] = a[2 * HALF :] + b[HALF : 2 * HALF]
        gr[n] = b[2 * HALF :].astype(gr.dtype)


def attention(meta, q, k, v, gm, left, right, earlier, off, heads):
    rows, width = q.shape

    def at(n, o):
        return pl.BlockSpec((n, HEAD_DIM), lambda h, s: (0, h + o))

    pair = pl.BlockSpec((2, HALF, HEAD_DIM), lambda h, s: (0, 0, h))
    w = heads * HEAD_DIM
    aliases = {7: 0, 8: 1} if earlier else {}
    return pl.pallas_call(
        attention_kernel,
        name="attention",
        out_shape=[
            SDS((rows, width), BF16),
            SDS((rows, width), BF16),
            SDS((rows, w), F32),
            SDS((rows, w), F32),
            SDS((2, HALF, w), BF16),
            SDS((2, HALF, w), BF16),
        ],
        grid_spec=pltpu.PrefetchScalarGridSpec(
            num_scalar_prefetch=1,
            grid=(heads,),
            in_specs=[at(rows, off)] * 4 + [pair] * 2 + [ANY] * len(earlier),
            out_specs=[at(rows, off)] * 2 + [at(rows, 0)] * 2 + [pair] * 2,
            scratch_shapes=[pltpu.VMEM((rows // HALF, HALF, 3 * HALF), F32)],
        ),
        input_output_aliases=aliases,
        compiler_params=pltpu.CompilerParams(dimension_semantics=("arbitrary",)),
    )(meta, q, k, v, gm, left, right, *earlier)


def join_kernel(dk, dv, low, high, *refs):
    for n, (own, out) in enumerate(zip((dk, dv), refs[-2:])):
        out[0:HALF] = (own[0:HALF] + low[n].astype(F32)).astype(out.dtype)
        out[HALF:] = (own[HALF:] + high[n].astype(F32)).astype(out.dtype)


def join(dk, dv, low, high, earlier, off, width, block=256):
    rows, w = dk.shape
    own = pl.BlockSpec((rows, block), lambda i: (0, i))
    pair = pl.BlockSpec((2, HALF, block), lambda i: (0, 0, i))
    out = pl.BlockSpec((rows, block), lambda i: (0, i + off // block))
    return pl.pallas_call(
        join_kernel,
        name="join",
        out_shape=[SDS((rows, width), BF16)] * 2,
        grid=(w // block,),
        in_specs=[own] * 2 + [pair] * 2 + [ANY] * len(earlier),
        out_specs=[out] * 2,
        input_output_aliases={4: 0, 5: 1} if earlier else {},
    )(dk, dv, low, high, *earlier)


def weight_kernel(core, go, att, keep, send, total):
    total[...] = dot_tn(go[...], att[...])
    n = keep.shape[1] // 2
    for i in range(2):
        mine = pl.multiple_of((2 * i + core[0]) * n, n)
        theirs = pl.multiple_of((2 * i + 1 - core[0]) * n, n)
        keep[0, i * n : (i + 1) * n] = total[pl.ds(mine, n)]
        send[0, i * n : (i + 1) * n] = total[pl.ds(theirs, n)].astype(send.dtype)


def weight_parts(core, go, att, off, heads):
    rows, width = go.shape
    wide = heads * HEAD_DIM
    half = pl.BlockSpec((1, width // 8, wide), lambda y, s: (y, 0, 0))
    return pl.pallas_call(
        weight_kernel,
        name="weight",
        out_shape=[SDS((4, width // 8, wide), F32), SDS((4, width // 8, wide), BF16)],
        grid_spec=pltpu.PrefetchScalarGridSpec(
            num_scalar_prefetch=1,
            grid=(4,),
            in_specs=[
                pl.BlockSpec((rows, width // 4), lambda y, s: (0, y)),
                pl.BlockSpec((rows, wide), lambda y, s: (0, off // heads)),
            ],
            out_specs=[half, half],
            scratch_shapes=[pltpu.VMEM((width // 4, wide), F32)],
        ),
    )(core, go, att)


def part_kernel(y, keep, got, own, *outs):
    k = pl.program_id(0)
    total = keep[0] + got[0].astype(F32)

    @pl.when(k == 0)
    def _():
        own[...] = total

    for n, out in enumerate(outs):

        @pl.when(k == n + 1)
        def _(out=out):
            out[...] = total.astype(out.dtype)


def parted(y, keep, got):
    _, n, wide = keep.shape
    turned = pl.BlockSpec((1, n, wide), lambda k, s: (lax.rem(s[0] + k, 4), 0, 0))
    fixed = pl.BlockSpec((n, wide), lambda k, s: (0, 0))
    return pl.pallas_call(
        part_kernel,
        name="parted",
        out_shape=[SDS((n, wide), F32)] + [SDS((n, wide), BF16)] * 3,
        grid_spec=pltpu.PrefetchScalarGridSpec(
            num_scalar_prefetch=1,
            grid=(4,),
            in_specs=[turned, turned],
            out_specs=[fixed] * 4,
        ),
    )(y, keep, got)


def passed(value, axis, by):
    devices = lax.axis_size(axis)
    pairs = [(i, i + by) for i in range(devices) if 0 <= i + by < devices]
    return lax.ppermute(value, axis, pairs)


def turned(value, axis, by):
    devices = lax.axis_size(axis)
    return lax.ppermute(value, axis, [(i, (i + by) % devices) for i in range(devices)])


def mixed_kernel(place, go, *refs):
    pieces, (out, weight, sems) = refs[:8], refs[8:]
    y, core = place[0], place[1]
    copies = []
    for n, piece in enumerate(pieces):
        side = core if n < 4 else 1 - core
        copies.append(
            pltpu.make_async_copy(
                piece, weight.at[lax.rem(y + 4 - n % 4, 4), :, side], sems.at[n]
            )
        )
    for copy in copies:
        copy.start()
    for copy in copies:
        copy.wait()
    out[...] = dot_nn(go[...], weight[...].reshape(go.shape[1], -1)).astype(out.dtype)


def mixed(place, go, pieces):
    rows, width = go.shape
    whole = pl.BlockSpec((rows, width), lambda i, s: (0, 0))
    return pl.pallas_call(
        mixed_kernel,
        name="mixed",
        out_shape=SDS((rows, width), BF16),
        grid_spec=pltpu.PrefetchScalarGridSpec(
            num_scalar_prefetch=1,
            grid=(1,),
            in_specs=[whole] + [ANY] * 8,
            out_specs=whole,
            scratch_shapes=[
                pltpu.VMEM((4, 2, 2) + pieces[0].shape[1:], BF16),
                pltpu.SemaphoreType.DMA((8,)),
            ],
        ),
    )(place, go, *pieces)


def swapped(value, bit):
    return lax.ppermute(value, "dp", [(i, i ^ bit) for i in range(lax.axis_size("dp"))])


def gathered(shard):
    low = (lax.axis_index("dp") // 2) % 2 == 0
    other = swapped(shard, 2)
    mine = [jnp.stack([jnp.where(low, shard, other), jnp.where(low, other, shard)])]
    for n in (1, 2, 3):
        mine.append(turned(mine[0], "dp", 4 * n))
    theirs = []
    for piece in mine:
        theirs.append(swapped(piece, 1))
    return mine + theirs


def deal_kernel(z, *refs):
    *ins, spread = refs
    own, *outs = ins[-8:]
    ins = ins[:-8]
    n = own.shape[1]
    off = 0
    for chunk in range(0, len(ins), 4):
        first, *rest = ins[chunk : chunk + 4]
        total = first[...]
        for got in rest:
            total = total + got[...].astype(F32)
        wide = total.shape[1]
        for x in range(2):
            for k in range(8):
                row = (x * 8 + k) * n
                spread[x, k, 0:n, off : off + wide] = total[row : row + n]
        off += wide
    for k, out in enumerate((own, *outs)):
        for x in range(2):
            out[x] = spread[x, lax.rem(z[0] + k, 8), 0:n].astype(out.dtype)


def deal(z, parts, width):
    rows = parts[0].shape[0] // 16
    shape = (2, rows, width)
    return pl.pallas_call(
        deal_kernel,
        name="deal",
        out_shape=[SDS(shape, F32)] + [SDS(shape, BF16)] * 7,
        grid_spec=pltpu.PrefetchScalarGridSpec(
            num_scalar_prefetch=1,
            grid=(1,),
            in_specs=[pl.BlockSpec(p.shape, lambda i, s: (0, 0)) for p in parts],
            out_specs=[pl.BlockSpec(shape, lambda i, s: (0, 0, 0))] * 8,
            scratch_shapes=[pltpu.VMEM((2, 8, 16, width), F32)],
        ),
    )(z, *parts)


def quarter_kernel(place, own, *refs):
    gots, outs = refs[:7], refs[7:]
    total = own[...]
    for got in gots:
        total = total + got[...].astype(F32)
    n = outs[0].shape[0]
    quarters = [[total[x, h * n : (h + 1) * n] for h in range(2)] for x in range(2)]
    for k, out in enumerate(outs):
        x, h = place[0] ^ (k // 2), place[1] ^ (k % 2)
        low = jnp.where(h == 0, quarters[0][0], quarters[0][1])
        high = jnp.where(h == 0, quarters[1][0], quarters[1][1])
        out[...] = jnp.where(x == 0, low, high)


def quartered(place, own, gots):
    _, rows, width = own.shape
    whole = pl.BlockSpec(own.shape, lambda i, s: (0, 0, 0))
    part = pl.BlockSpec((rows // 2, width), lambda i, s: (0, 0))
    return pl.pallas_call(
        quarter_kernel,
        name="quarter",
        out_shape=[SDS((rows // 2, width), F32)] * 4,
        grid_spec=pltpu.PrefetchScalarGridSpec(
            num_scalar_prefetch=1, grid=(1,), in_specs=[whole] * 8, out_specs=[part] * 4
        ),
    )(place, own, *gots)


def crossed(value, k):
    count = lax.axis_size("seq")
    pairs = [
        (d * count + s, (d ^ (k // 2 * 2)) * count + (s ^ (k % 2)))
        for d in range(lax.axis_size("dp"))
        for s in range(count)
    ]
    return lax.ppermute(value, ("dp", "seq"), pairs)


CHUNKS = (8, 4)


def step(queries, keys, values, grad_out, out_weight, lengths):
    rows, width = queries.shape
    first_row = lax.axis_index("seq") * rows
    dp = lax.axis_index("dp")
    y, core = dp // 4, dp % 2
    meta = jnp.stack([first_row, lengths[0]]).astype(jnp.int32)
    offs = [sum(CHUNKS[:n]) for n in range(len(CHUNKS))]
    pieces = gathered(out_weight)
    halos = []
    for off, heads in zip(offs, CHUNKS):
        a, b = off * HEAD_DIM, (off + heads) * HEAD_DIM
        tail = jnp.stack([keys[rows - HALF :, a:b], values[rows - HALF :, a:b]])
        head = jnp.stack([keys[:HALF, a:b], values[:HALF, a:b]])
        left = passed(tail, "seq", 1)
        right = passed(head, "seq", -1)
        halos.append((left, right))
    grad_mixed = mixed(jnp.stack([y, core]).astype(jnp.int32), grad_out, pieces)
    earlier, sums, parts = (), [], []
    for (left, right), off, heads in zip(halos, offs, CHUNKS):
        att, dq, dk, dv, gl, gr = attention(
            meta, queries, keys, values, grad_mixed, left, right, earlier, off, heads
        )
        earlier = (att, dq)
        low = passed(gr, "seq", 1)
        high = passed(gl, "seq", -1)
        sums.append((dk, dv, low, high))
        keep, send = weight_parts(core[None], grad_out, att, off, heads)
        got = swapped(send, 1)
        own, *rest = parted(y[None], keep, got)
        gots = []
        for k, part in enumerate(rest):
            gots.append(turned(part, "dp", 4 * (k + 1)))
        parts += [own, *gots]
    seq = lax.axis_index("seq")
    own, *rest = deal((seq // 2)[None], parts, width)
    gots = []
    for k, part in enumerate(rest):
        gots.append(turned(part, "seq", 2 * (k + 1)))
    place = jnp.stack([(dp // 2) % 2, seq % 2]).astype(jnp.int32)
    own, *rest = quartered(place, own, gots)
    for k, part in enumerate(rest):
        own = own + crossed(part, k + 1)
    outs = ()
    for n, off in enumerate(offs):
        outs = tuple(join(*sums[n], outs, off * HEAD_DIM, width))
    return dq, outs[0], outs[1], own


def solution(mesh):
    rows = P(("dp", "seq"), None)
    return jax.shard_map(
        step,
        mesh=mesh,
        in_specs=(rows, rows, rows, rows, P("dp", None), P("dp")),
        out_specs=(rows, rows, rows, rows),
        check_vma=False,
    )
```

```python
import jax
import jax.numpy as jnp
from jax import lax
from jax.experimental import pallas as pl
from jax.experimental.pallas import tpu as pltpu
from jax.sharding import PartitionSpec as P


HEAD_DIM = 128
HALF = 256
LOG2E = 1.4426950408889634
F32 = jnp.float32
BF16 = jnp.bfloat16
ANY = pl.BlockSpec(memory_space=pl.ANY)
SDS = jax.ShapeDtypeStruct


def dot_nt(a, b):
    return lax.dot_general(a, b, (((1,), (1,)), ((), ())), preferred_element_type=F32)


def dot_nn(a, b):
    return lax.dot_general(a, b, (((1,), (0,)), ((), ())), preferred_element_type=F32)


def dot_tn(a, b):
    return lax.dot_general(a, b, (((0,), (0,)), ((), ())), preferred_element_type=F32)


def attention_kernel(meta, q, k, v, gm, left, right, *refs):
    att, dq, dk, dv, gl, gr, bias = refs[-7:]
    rows = q.shape[0]
    width = 3 * HALF
    scale = HEAD_DIM ** (-0.5)
    first_row = meta[0]
    length = meta[1]

    @pl.when(pl.program_id(0) == 0)
    def _():
        for b in range(rows // HALF):
            start = first_row + b * HALF
            r = lax.broadcasted_iota(jnp.int32, (HALF, width), 0)
            c = lax.broadcasted_iota(jnp.int32, (HALF, width), 1)
            u = c + (start - HALF)
            ok = (c >= r) & (c < r + 2 * HALF) & (u >= 0) & (u < length)
            bias[b] = jnp.where(ok, 0.0, -1e30)

    def products(cols, b):
        def window(n, own, ends):
            low = ends[0][n, :, cols] if b == 0 else own[0:HALF, cols]
            high = own[HALF:, cols] if b == 0 else ends[1][n, :, cols]
            middle = own[0:HALF, cols] if b == 0 else own[HALF:, cols]
            return jnp.concatenate([low, middle, high], axis=0)

        at = slice(b * HALF, (b + 1) * HALF)
        qb, gb = q[at, cols], gm[at, cols]
        kc, vc = window(0, k, (left, right)), window(1, v, (left, right))
        s = dot_nt(qb, kc) + bias[b]
        return cols, b, qb, gb, kc, vc, s, dot_nt(gb, vc)

    def softmax(cols, b, qb, gb, kc, vc, s, dp):
        m = jnp.max(s, axis=1, keepdims=True)
        e = jnp.exp2((s - m) * (scale * LOG2E))
        pos = first_row + b * HALF + lax.broadcasted_iota(jnp.int32, (HALF, 1), 0)
        total = jnp.maximum(jnp.sum(e, axis=1, keepdims=True), 1.0)
        p = e * jnp.where(pos < length, 1.0 / total, 0.0)
        delta = jnp.sum(p * dp, axis=1, keepdims=True)
        return cols, b, qb, gb, kc, vc, p.astype(BF16), (p * (dp - delta)).astype(BF16)

    terms = {}

    def gradients(cols, b, qb, gb, kc, vc, pb, ds):
        at = slice(b * HALF, (b + 1) * HALF)
        att[at, cols] = dot_nn(pb, vc).astype(att.dtype)
        dq[at, cols] = (dot_nn(ds, kc) * scale).astype(dq.dtype)
        terms[cols.start, b] = (dot_tn(ds, qb) * scale, dot_tn(pb, gb))

    tasks = [
        (slice(n * HEAD_DIM, (n + 1) * HEAD_DIM), b)
        for n in range(q.shape[1] // HEAD_DIM)
        for b in range(rows // HALF)
    ]
    ahead = products(*tasks[0])
    behind = None
    for n in range(len(tasks)):
        now, ahead = ahead, products(*tasks[n + 1]) if n + 1 < len(tasks) else None
        done = softmax(*now)
        if behind is not None:
            gradients(*behind)
        behind = done
    gradients(*behind)
    for cols in dict.fromkeys(task[0].start for task in tasks):
        for n, own in enumerate((dk, dv)):
            a, b = terms[cols, 0][n], terms[cols, 1][n]
            at = slice(cols, cols + HEAD_DIM)
            gl[n, :, at] = a[0:HALF].astype(gl.dtype)
            own[0:HALF, at] = a[HALF : 2 * HALF] + b[0:HALF]
            own[HALF:, at] = a[2 * HALF :] + b[HALF : 2 * HALF]
            gr[n, :, at] = b[2 * HALF :].astype(gr.dtype)


def attention(meta, q, k, v, gm, left, right, earlier, off, heads, starts, group_heads):
    rows, width = q.shape
    wide = 2 * HEAD_DIM

    def at(o):
        return pl.BlockSpec((rows, wide), lambda h, s: (0, h + o // 2))

    def pair(o):
        return pl.BlockSpec((2, HALF, wide), lambda h, s: (0, 0, h + o // 2))

    w = group_heads * HEAD_DIM
    return pl.pallas_call(
        attention_kernel,
        name="attention",
        out_shape=[
            SDS((rows, width), BF16),
            SDS((rows, width), BF16),
            SDS((rows, w), F32),
            SDS((rows, w), F32),
            SDS((2, HALF, w), BF16),
            SDS((2, HALF, w), BF16),
        ],
        grid_spec=pltpu.PrefetchScalarGridSpec(
            num_scalar_prefetch=1,
            grid=(heads // 2,),
            in_specs=[at(off)] * 3 + [at(starts[0])] + [pair(0)] * 2 + [ANY] * len(earlier),
            out_specs=[at(off)] * 2 + [at(starts[1])] * 2 + [pair(starts[1])] * 2,
            scratch_shapes=[pltpu.VMEM((rows // HALF, HALF, 3 * HALF), F32)],
        ),
        input_output_aliases={7 + n: n for n in range(len(earlier))},
        compiler_params=pltpu.CompilerParams(dimension_semantics=("arbitrary",)),
    )(meta, q, k, v, gm, left, right, *earlier)


def join_kernel(dk, dv, low, high, *refs):
    for n, (own, out) in enumerate(zip((dk, dv), refs[-2:])):
        out[0:HALF] = (own[0:HALF] + low[n].astype(F32)).astype(out.dtype)
        out[HALF:] = (own[HALF:] + high[n].astype(F32)).astype(out.dtype)


def join(dk, dv, low, high, earlier, off, width, block=256):
    rows, w = dk.shape
    own = pl.BlockSpec((rows, block), lambda i: (0, i))
    pair = pl.BlockSpec((2, HALF, block), lambda i: (0, 0, i))
    out = pl.BlockSpec((rows, block), lambda i: (0, i + off // block))
    return pl.pallas_call(
        join_kernel,
        name="join",
        out_shape=[SDS((rows, width), BF16)] * 2,
        grid=(w // block,),
        in_specs=[own] * 2 + [pair] * 2 + [ANY] * len(earlier),
        out_specs=[out] * 2,
        input_output_aliases={4: 0, 5: 1} if earlier else {},
    )(dk, dv, low, high, *earlier)


def weight_kernel(core, go, att, keep, send, total):
    total[...] = dot_tn(go[...], att[...])
    n = keep.shape[1] // 2
    for i in range(2):
        mine = pl.multiple_of((2 * i + core[0]) * n, n)
        theirs = pl.multiple_of((2 * i + 1 - core[0]) * n, n)
        keep[0, i * n : (i + 1) * n] = total[pl.ds(mine, n)]
        send[0, i * n : (i + 1) * n] = total[pl.ds(theirs, n)].astype(send.dtype)


def weight_parts(core, go, att, off, heads):
    rows, width = go.shape
    wide = heads * HEAD_DIM
    half = pl.BlockSpec((1, width // 8, wide), lambda y, s: (y, 0, 0))
    return pl.pallas_call(
        weight_kernel,
        name="weight",
        out_shape=[SDS((4, width // 8, wide), F32), SDS((4, width // 8, wide), BF16)],
        grid_spec=pltpu.PrefetchScalarGridSpec(
            num_scalar_prefetch=1,
            grid=(4,),
            in_specs=[
                pl.BlockSpec((rows, width // 4), lambda y, s: (0, y)),
                pl.BlockSpec((rows, wide), lambda y, s: (0, off // heads)),
            ],
            out_specs=[half, half],
            scratch_shapes=[pltpu.VMEM((width // 4, wide), F32)],
        ),
    )(core, go, att)


def part_kernel(y, keep, got, own, *outs):
    k = pl.program_id(0)
    total = keep[0] + got[0].astype(F32)

    @pl.when(k == 0)
    def _():
        own[...] = total

    for n, out in enumerate(outs):

        @pl.when(k == n + 1)
        def _(out=out):
            out[...] = total.astype(out.dtype)


def parted(y, keep, got):
    _, n, wide = keep.shape
    turned = pl.BlockSpec((1, n, wide), lambda k, s: (lax.rem(s[0] + k, 4), 0, 0))
    fixed = pl.BlockSpec((n, wide), lambda k, s: (0, 0))
    return pl.pallas_call(
        part_kernel,
        name="parted",
        out_shape=[SDS((n, wide), F32)] + [SDS((n, wide), BF16)] * 3,
        grid_spec=pltpu.PrefetchScalarGridSpec(
            num_scalar_prefetch=1,
            grid=(4,),
            in_specs=[turned, turned],
            out_specs=[fixed] * 4,
        ),
    )(y, keep, got)


def passed(value, axis, by):
    devices = lax.axis_size(axis)
    pairs = [(i, i + by) for i in range(devices) if 0 <= i + by < devices]
    return lax.ppermute(value, axis, pairs)


def turned(value, axis, by):
    devices = lax.axis_size(axis)
    return lax.ppermute(value, axis, [(i, (i + by) % devices) for i in range(devices)])


def mixed_kernel(place, go, *refs):
    pieces, (out, weight, sems) = refs[:8], refs[8:]
    y, core = place[0], place[1]
    copies = []
    for n, piece in enumerate(pieces):
        side = core if n < 4 else 1 - core
        copies.append(
            pltpu.make_async_copy(
                piece, weight.at[lax.rem(y + 4 - n % 4, 4), :, side], sems.at[n]
            )
        )
    for copy in copies:
        copy.start()
    for copy in copies:
        copy.wait()
    out[...] = dot_nn(go[...], weight[...].reshape(go.shape[1], -1)).astype(out.dtype)


def mixed(place, go, pieces):
    rows, width = go.shape
    cols = pieces[0].shape[-1]
    return pl.pallas_call(
        mixed_kernel,
        name="mixed",
        out_shape=SDS((rows, cols), BF16),
        grid_spec=pltpu.PrefetchScalarGridSpec(
            num_scalar_prefetch=1,
            grid=(1,),
            in_specs=[pl.BlockSpec((rows, width), lambda i, s: (0, 0))] + [ANY] * 8,
            out_specs=pl.BlockSpec((rows, cols), lambda i, s: (0, 0)),
            scratch_shapes=[
                pltpu.VMEM((4, 2, 2) + pieces[0].shape[1:], BF16),
                pltpu.SemaphoreType.DMA((8,)),
            ],
        ),
    )(place, go, *pieces)


def swapped(value, bit):
    return lax.ppermute(value, "dp", [(i, i ^ bit) for i in range(lax.axis_size("dp"))])


def gathered(shard, cuts):
    low = (lax.axis_index("dp") // 2) % 2 == 0
    other = swapped(shard, 2)
    groups = []
    for a, b in cuts:
        own, far = shard[:, a:b], other[:, a:b]
        mine = [jnp.stack([jnp.where(low, own, far), jnp.where(low, far, own)])]
        for n in (1, 2, 3):
            mine.append(turned(mine[0], "dp", 4 * n))
        theirs = []
        for piece in mine:
            theirs.append(swapped(piece, 1))
        groups.append(mine + theirs)
    return groups


def deal_kernel(*refs):
    *ins, out, spread = refs
    count, rows, _ = out.shape
    n = rows // 2
    off = 0
    for chunk in range(0, len(ins), 4):
        first, *rest = ins[chunk : chunk + 4]
        total = first[...]
        for got in rest:
            total = total + got[...].astype(F32)
        wide = total.shape[1]
        for x in range(2):
            for k in range(count):
                row = (x * count + k) * n
                spread[k, x * n : (x + 1) * n, off : off + wide] = total[row : row + n]
        off += wide
    out[...] = spread[...].astype(out.dtype)


def deal(parts, count, width):
    shape = (count, parts[0].shape[0] // count, width)
    return pl.pallas_call(
        deal_kernel,
        name="deal",
        out_shape=SDS(shape, BF16),
        grid=(1,),
        in_specs=[pl.BlockSpec(p.shape, lambda i: (0, 0)) for p in parts],
        out_specs=pl.BlockSpec(shape, lambda i: (0, 0, 0)),
        scratch_shapes=[pltpu.VMEM(shape, F32)],
    )(*parts)


def quarter_kernel(place, got, *outs):
    total = got[0].astype(F32)
    for k in range(1, got.shape[0]):
        total = total + got[k].astype(F32)
    n = outs[0].shape[0]
    quarters = [total[i * n : (i + 1) * n] for i in range(4)]
    for k, out in enumerate(outs):
        x, h = place[0] ^ (k // 2), place[1] ^ (k % 2)
        low = jnp.where(h == 0, quarters[0], quarters[1])
        high = jnp.where(h == 0, quarters[2], quarters[3])
        out[...] = jnp.where(x == 0, low, high)


def quartered(place, got):
    _, rows, width = got.shape
    part = pl.BlockSpec((rows // 4, width), lambda i, s: (0, 0))
    return pl.pallas_call(
        quarter_kernel,
        name="quarter",
        out_shape=[SDS((rows // 4, width), F32)] * 4,
        grid_spec=pltpu.PrefetchScalarGridSpec(
            num_scalar_prefetch=1,
            grid=(1,),
            in_specs=[pl.BlockSpec(got.shape, lambda i, s: (0, 0, 0))],
            out_specs=[part] * 4,
        ),
    )(place, got)


def crossed(value, k):
    count = lax.axis_size("seq")
    pairs = [
        (d * count + s, (d ^ (k // 2 * 2)) * count + (s ^ (k % 2)))
        for d in range(lax.axis_size("dp"))
        for s in range(count)
    ]
    return lax.ppermute(value, ("dp", "seq"), pairs)


CHUNKS = (8, 4)
GROUPS = ((0,), (1,))
MIXED = ((0, 1),)


def step(queries, keys, values, grad_out, out_weight, lengths):
    rows, width = queries.shape
    first_row = lax.axis_index("seq") * rows
    dp, seq = lax.axis_index("dp"), lax.axis_index("seq")
    y, core = dp // 4, dp % 2
    meta = jnp.stack([first_row, lengths[0]]).astype(jnp.int32)
    offs = [sum(CHUNKS[:n]) for n in range(len(CHUNKS) + 1)]
    cuts = [(offs[m[0]] * HEAD_DIM, offs[m[-1] + 1] * HEAD_DIM) for m in MIXED]
    weights = gathered(out_weight, cuts)
    halos = []
    for n in range(len(CHUNKS)):
        a, b = offs[n] * HEAD_DIM, offs[n + 1] * HEAD_DIM
        tail = jnp.stack([keys[rows - HALF :, a:b], values[rows - HALF :, a:b]])
        head = jnp.stack([keys[:HALF, a:b], values[:HALF, a:b]])
        left = passed(tail, "seq", 1)
        right = passed(head, "seq", -1)
        halos.append((left, right))
    mixes = {}
    for g, chunks in enumerate(MIXED):
        part = mixed(jnp.stack([y, core]).astype(jnp.int32), grad_out, weights[g])
        for n in chunks:
            mixes[n] = part, offs[n] - offs[chunks[0]]
    whole, sums, parts = (), [], []
    for chunks in GROUPS:
        off, heads = offs[chunks[0]], sum(CHUNKS[n] for n in chunks)
        terms = ()
        for n in chunks:
            part, start = mixes[n]
            made = attention(
                meta, queries, keys, values, part, *halos[n], whole + terms,
                offs[n], CHUNKS[n], (start, offs[n] - off), heads,
            )
            whole, terms = tuple(made[:2]), tuple(made[2:])
        dk, dv, gl, gr = terms
        low = passed(gr, "seq", 1)
        high = passed(gl, "seq", -1)
        sums.append((dk, dv, low, high))
        keep, send = weight_parts(core[None], grad_out, whole[0], off, heads)
        got = swapped(send, 1)
        own, *rest = parted(y[None], keep, got)
        gots = []
        for k, part in enumerate(rest):
            gots.append(turned(part, "dp", 4 * (k + 1)))
        parts += [own, *gots]
    count = lax.axis_size("seq")
    dealt = deal(parts, count // 2, width)
    rings = [list(range(k, count, 2)) for k in range(2)]
    got = lax.all_to_all(dealt, "seq", 0, 0, tiled=True, axis_index_groups=rings)
    place = jnp.stack([(dp // 2) % 2, seq % 2]).astype(jnp.int32)
    own, *rest = quartered(place, got)
    for k, part in enumerate(rest):
        own = own + crossed(part, k + 1)
    outs = ()
    for g, chunks in enumerate(GROUPS):
        outs = tuple(join(*sums[g], outs, offs[chunks[0]] * HEAD_DIM, width))
    return whole[1], outs[0], outs[1], own


def solution(mesh):
    rows = P(("dp", "seq"), None)
    return jax.shard_map(
        step,
        mesh=mesh,
        in_specs=(rows, rows, rows, rows, P("dp", None), P("dp")),
        out_specs=(rows, rows, rows, rows),
        check_vma=False,
    )
```
